256 devices in a mesh: pipe: 2 (over core), expert: 16 (over y, x), dp: 8 (over z).
Axes of the slice: x: 4, y: 4, z: 8, core: 2. Of those that a mesh axis runs over, the one named last changes fastest.
Arguments:
- tokens: bfloat16 [2048, 6144], P('expert'), may hold values from -6 to 6
- expert_ids: int32 [2048, 2], P('expert'), may hold values from 0 to 15, all different within a row; in each aligned block of 128 rows (0 to 127, 128 to 255, ...) at most 24 rows name the same one
- w_router: bfloat16 [6144, 16], replicated, may hold values from -0.078125 to 0.078125
- w_gate: bfloat16 [16, 6144, 4096], P('expert', None, ('pipe', 'dp')), may hold values from -0.078125 to 0.078125
- w_up: bfloat16 [16, 6144, 4096], P('expert', None, ('pipe', 'dp')), may hold values from -0.078125 to 0.078125
- w_down: bfloat16 [16, 4096, 6144], P('expert', ('pipe', 'dp')), may hold values from -0.125 to 0.125
Outputs:
- mixed: bfloat16 [2048, 6144], P('expert', ('pipe', 'dp'))
The draws below stay inside these ranges and needn't reach their ends.
Inputs may be any that keep to these rules, and one draw needn't show every extreme that they name: `expert_ids`: in each aligned block of 128 tokens no expert is named by more than 24 of the block's choices, a bound that some block reaches; the two experts of a token differ.
All inputs are finite; a program needn't handle non-finite values.
Results may differ from the reference program's by a relative error of at most 0.018.
Values may be sent and summed in bfloat16 or wider, within the bound.
A program may use at most 64 MiB of HBM per device.

```python
import math
import jax
import jax.numpy as jnp
import numpy as np
from jax import lax

D = 6144
FF_DEV = 256
TOPK = 2
TOK_DEV = 128
EXPERTS = 16
FF = 4096
CAP = 24
TOKENS = 2048


def spiked(array, key, source, target, parts, factor):
    def block_of(position):
        return (jnp.arange(array.shape[position]) // (array.shape[position] // parts)).reshape((-1,) + (1,) * (array.ndim - 1 - position))

    first = jax.random.permutation(key, parts)[block_of(target)]
    far = (block_of(target) + parts // 2) % parts
    return jnp.where((block_of(source) == first) | (block_of(source) == far), factor * array, array)


def steps_of(key, extent, pieces, low, high):
    loudness, own = 1.0, jax.random.fold_in(key, 6)
    for dim, blocks in pieces:
        heights = jnp.exp(jax.random.uniform(jax.random.fold_in(own, dim), (blocks,), jnp.float32, low / len(pieces), high / len(pieces)))
        loudness = loudness * jnp.repeat(heights, extent[dim] // blocks).reshape([-1 if axis == dim else 1 for axis in range(len(extent))])
    return loudness


def shared_out(own_key, own, number, rows, count, top, reach, skew):
    sequence = jax.random.permutation(own_key, count)
    crowded, ordinary = shares(count, rows * top, reach, skew, True), shares(count, rows * top, reach, skew, False)
    places = jnp.arange(count)

    def named(sizes, turn):
        used = int((sizes > 0).sum())
        fixed = max(1, used // 4)
        passed = fixed + (places - fixed + turn * (used - fixed)) % max(1, count - fixed)
        return jnp.zeros((count,), jnp.int32).at[sequence[jnp.where(places < fixed, places, passed)]].set(jnp.asarray(sizes, jnp.int32))

    sizes = jnp.where(number % 4 == 0, named(crowded, number // 4), named(ordinary, number - number // 4 - 1))
    mixed = jax.random.permutation(jax.random.fold_in(own, 3), count)
    donor, receiver = mixed[0:count // 2 * 2:2], mixed[1:count // 2 * 2:2]
    margin = jnp.minimum(sizes[donor] - 1, reach - sizes[receiver]) // 2
    margin = jnp.where((donor == sequence[0]) | (receiver == sequence[0]) | (sizes[receiver] == 0), 0, jnp.maximum(margin, 0))
    passed = jax.random.randint(jax.random.fold_in(own, 4), (count // 2,), 0, 1 << 20) % (margin + 1)
    sizes = sizes.at[donor].add(-passed).at[receiver].add(passed)
    labels = jnp.searchsorted(jnp.cumsum(sizes), jnp.arange(rows * top), side="right").astype(jnp.int32)
    table = labels.reshape(top, rows).T
    table = table[jax.random.permutation(jax.random.fold_in(own, 1), rows)]
    turn = jax.random.randint(jax.random.fold_in(own, 2), (rows, 1), 0, top)
    return jnp.take_along_axis(table, (jnp.arange(top)[None, :] + turn) % top, axis=1)


def shares(number_of, total, limit, lean, full):
    loads = [(1 << 20) // math.isqrt(grade ** lean) + 1 for grade in range(1, number_of + 1)]
    largest = limit if full else min(limit, max(-(-total // number_of), total * loads[0] // sum(loads)))
    least = 1 if total - largest >= number_of - 1 else 0
    holding, surplus = [largest] + [least] * (number_of - 1), total - largest - least * (number_of - 1)
    while surplus > 0:
        candidates = [i for i in range(1, number_of) if holding[i] < largest] or [i for i in range(1, number_of) if holding[i] < limit]
        mass, budget = sum([loads[i] for i in candidates]), surplus
        for i in candidates:
            addition = min(limit - holding[i], max(1, budget * loads[i] // mass), surplus)
            holding[i] = holding[i] + addition
            surplus = surplus - addition
    return np.array(holding)


def gaussian(rng, shape, deviation, most, pieces=(), kind=jnp.bfloat16):
    loudness = steps_of(rng, shape, pieces, -0.22, 0.18) if pieces else 1.0
    entries = jax.random.normal(rng, shape, jnp.float32) * deviation * loudness
    return jnp.minimum(jnp.maximum(entries, -most), most).astype(kind)


def noise_with(key, extent, deviation, reach, shards, heavy, kind=jnp.bfloat16):
    values = deviation * jax.random.normal(key, extent, jnp.float32)
    if shards:
        values = values * steps_of(key, extent, shards, -0.22, 0.18)
    return jnp.clip(spiked(values, jax.random.fold_in(key, 3), *heavy), -reach, reach).astype(kind)


def setup_inputs(seed: int = 0) -> dict:
    streams_of = jax.random.split(jax.random.key(seed), 7)
    tokens = gaussian(streams_of[0], (TOKENS, D), 1.0, 6.0, ((0, 16),))
    expert_ids_keys = jax.random.split(jax.random.fold_in(streams_of[1], 1), TOKENS // TOK_DEV)
    expert_ids_turns = jax.random.permutation(jax.random.fold_in(streams_of[1], 3), TOKENS // TOK_DEV)
    expert_ids = jax.vmap(lambda own, number: shared_out(jax.random.fold_in(streams_of[1], 2), own, number, TOK_DEV, EXPERTS, TOPK, CAP, 2))(expert_ids_keys, expert_ids_turns).reshape((TOKENS, TOPK))
    w_router = gaussian(streams_of[2], (D, EXPERTS), D ** -0.5, 0.078125)
    w_gate = gaussian(streams_of[3], (EXPERTS, D, FF), D ** -0.5, 0.078125, ((0, 16), (2, 16)))
    w_up = gaussian(streams_of[4], (EXPERTS, D, FF), D ** -0.5, 0.078125, ((0, 16), (2, 16)))
    w_down = noise_with(streams_of[5], (EXPERTS, FF, D), FF ** -0.5, 0.125, ((0, 16), (1, 16)), (1, 2, 16, 2.0))
    return dict(tokens=tokens, expert_ids=expert_ids, w_router=w_router, w_gate=w_gate, w_up=w_up, w_down=w_down)


def slots_of(ids):
    blocks = ids.shape[0]
    flat = ids.reshape(blocks, -1).astype(jnp.int32)
    onehot = (flat[:, :, None] == jnp.arange(EXPERTS, dtype=jnp.int32)[None, None, :]).astype(jnp.int32)
    before = jnp.cumsum(onehot, axis=1) - onehot
    slot = jnp.sum(before * onehot, axis=-1).astype(jnp.int32)
    return flat, slot


def expert_rows(inputs, wg, wu, wd):
    gate = jnp.dot(inputs, wg, preferred_element_type=jnp.float32)
    upper = jnp.dot(inputs, wu, preferred_element_type=jnp.float32)
    hidden = (jax.nn.silu(gate) * upper).astype(jnp.bfloat16)
    groups = FF // FF_DEV
    hidden_groups = jnp.transpose(hidden.reshape(inputs.shape[0], groups, FF_DEV), (1, 0, 2))
    down_groups = wd.reshape(groups, FF_DEV, D)

    def add_group(total, pair):
        part = jnp.dot(pair[0], pair[1], preferred_element_type=jnp.float32).astype(jnp.bfloat16)
        return total + part.astype(jnp.float32), None

    total, _ = lax.scan(add_group, jnp.zeros((inputs.shape[0], D), jnp.float32), (hidden_groups, down_groups))
    return total.astype(jnp.bfloat16)


def reference(tokens, expert_ids, w_router, w_gate, w_up, w_down):
    blocks = TOKENS // TOK_DEV
    x_blocks = tokens.reshape(blocks, TOK_DEV, D)
    flat, slot = slots_of(expert_ids.reshape(blocks, TOK_DEV, TOPK))
    dest = flat * CAP + slot
    repeated = jnp.repeat(x_blocks, TOPK, axis=1)
    block_index = jnp.arange(blocks, dtype=jnp.int32)[:, None]
    buffer = jnp.zeros((blocks, EXPERTS * CAP, D), jnp.bfloat16)
    buffer = buffer.at[block_index, dest].set(repeated)
    buffer = buffer.reshape(blocks, EXPERTS, CAP, D)

    def one_expert(index):
        inputs = lax.dynamic_index_in_dim(buffer, index, 1, keepdims=False).reshape(blocks * CAP, D)
        wg = lax.dynamic_index_in_dim(w_gate, index, 0, keepdims=False)
        wu = lax.dynamic_index_in_dim(w_up, index, 0, keepdims=False)
        wd = lax.dynamic_index_in_dim(w_down, index, 0, keepdims=False)
        return expert_rows(inputs, wg, wu, wd).reshape(blocks, CAP, D)

    outputs = lax.map(one_expert, jnp.arange(EXPERTS, dtype=jnp.int32))
    logits = jnp.dot(tokens, w_router, preferred_element_type=jnp.float32)
    chosen = jnp.take_along_axis(logits, expert_ids.astype(jnp.int32), axis=1)
    first = jax.nn.sigmoid(chosen[:, 0] - chosen[:, 1])
    gates = jnp.stack([first, 1.0 - first], axis=1)
    picked = outputs[flat, jnp.broadcast_to(block_index, flat.shape), slot]
    picked = picked.reshape(TOKENS, TOPK, D).astype(jnp.float32)
    return jnp.sum(gates[:, :, None] * picked, axis=1).astype(jnp.bfloat16)
```

```python
import jax
import jax.numpy as jnp
from jax import lax
from jax.sharding import PartitionSpec as P


def slots_of(ids, experts):
    blocks = ids.shape[0]
    flat = ids.reshape(blocks, -1)
    onehot = (flat[:, :, None] == jnp.arange(experts, dtype=jnp.int32)[None, None, :]).astype(
        jnp.int32
    )
    before = jnp.cumsum(onehot, axis=1) - onehot
    slot = jnp.sum(before * onehot, axis=-1)
    return (flat, slot)


def dispatch(x_rows, id_rows, experts, capacity):
    count, width = x_rows.shape
    topk = id_rows.shape[1]
    flat, slot = slots_of(id_rows[None], experts)
    dest = flat[0] * capacity + slot[0]
    select = (jnp.arange(experts * capacity, dtype=jnp.int32)[:, None] == dest[None, :]).astype(
        jnp.bfloat16
    )
    repeated = jnp.repeat(x_rows, topk, axis=0)
    placed = jnp.dot(select, repeated, preferred_element_type=jnp.float32).astype(jnp.bfloat16)
    return (placed.reshape(experts, capacity, width), dest)


def body(tokens, expert_ids, w_router, w_gate, w_up, w_down):
    count, width = tokens.shape
    topk = expert_ids.shape[1]
    experts = lax.axis_size("expert") * w_gate.shape[0]
    capacity = 3 * count * topk // (2 * experts)
    groups = lax.axis_size(("pipe", "dp"))
    columns = width // groups
    start = lax.axis_index(("pipe", "dp")) * columns
    mine = lax.dynamic_slice_in_dim(tokens, start, columns, 1)
    local, dest = dispatch(mine, expert_ids, experts, capacity)
    arrived = lax.all_to_all(local, "expert", split_axis=0, concat_axis=0, tiled=True)
    arrived = arrived.reshape(experts * capacity, columns)
    inputs = lax.all_gather(arrived, ("pipe", "dp"), axis=1, tiled=True)
    gate = jnp.dot(inputs, w_gate[0], preferred_element_type=jnp.float32)
    upper = jnp.dot(inputs, w_up[0], preferred_element_type=jnp.float32)
    hidden = (jax.nn.silu(gate) * upper).astype(jnp.bfloat16)
    term = jnp.dot(hidden, w_down[0], preferred_element_type=jnp.float32).astype(jnp.bfloat16)
    logits = jnp.dot(tokens, w_router, preferred_element_type=jnp.float32)
    chosen = jnp.take_along_axis(logits, expert_ids, axis=1)
    first = jax.nn.sigmoid(chosen[:, 0] - chosen[:, 1])
    gates = jnp.stack([first, 1.0 - first], axis=1)
    summed = lax.psum_scatter(term, ("pipe", "dp"), scatter_dimension=1, tiled=True)
    returned = lax.all_to_all(
        summed.reshape(experts, capacity, columns), "expert", split_axis=0, concat_axis=0, tiled=True
    )
    picked = jnp.take(returned.reshape(experts * capacity, columns), dest, axis=0)
    picked = picked.reshape(count, topk, columns).astype(jnp.float32)
    return jnp.sum(gates[:, :, None] * picked, axis=1).astype(jnp.bfloat16)


def solution(mesh):
    placed = (
        P("expert", None),
        P("expert", None),
        P(),
        P("expert", None, ("pipe", "dp")),
        P("expert", None, ("pipe", "dp")),
        P("expert", ("pipe", "dp"), None),
    )
    return jax.shard_map(
        body, mesh=mesh, in_specs=placed, out_specs=P("expert", ("pipe", "dp")), check_vma=False
    )
```
